128 devices in a mesh: inp: 2 (over z_hi), tm: 64 (over z_lo, x, y, core).
Axes of the slice: x: 4, y: 4, z: 4 (z_hi: 2, z_lo: 2; z = z_hi * 2 + z_lo), core: 2. Of those that a mesh axis runs over, the one named last changes fastest.
Arguments:
- raw: bfloat16 [1024, 524288], P('inp', 'tm'), may hold values from -6 to 6
- taps: float32 [4, 512], replicated, may hold values from -3 to 3
Outputs:
- visibilities: float32 [256, 2, 1024, 1024], P('tm', None, 'inp')
The draws below stay inside these ranges and needn't reach their ends.
All inputs are finite; a program needn't handle non-finite values.
Results may differ from the reference program's by a relative error of at most 0.0052.
Values may be sent and summed in bfloat16 or wider, within the bound.
A program may use at most 192 MiB of HBM per device.

```python
import math
import jax
import jax.numpy as jnp
from jax import lax

NI = 1024
NFFT = 512
TAPS = 4
NCH = 256
NSPEC = 1024
NSAMP = 524288


def shard_levels(stream_key, dims, shards, smallest, top_value):
    def one(position, parts):
        draws = jax.random.uniform(jax.random.fold_in(jax.random.fold_in(stream_key, 6), position), (parts,), jnp.float32, smallest / len(shards), top_value / len(shards))
        return jnp.repeat(jnp.exp(draws), dims[position] // parts).reshape((-1,) + (1,) * (len(dims) - position - 1))

    level = one(*shards[0])
    for cut in shards[1:]:
        level = level * one(*cut)
    return level


def normal_values(stream_key, extent, spread, bound, cuts=(), held_as=jnp.bfloat16):
    array = jax.random.normal(stream_key, extent, jnp.float32) * spread
    if len(cuts) > 0:
        array = shard_levels(stream_key, extent, cuts, -0.22, 0.18) * array
    return jnp.clip(array, min=-bound, max=bound).astype(held_as)


def setup_inputs(seed: int = 0) -> dict:
    streams_of = jax.random.split(jax.random.key(seed), 3)
    return {
        "raw": normal_values(streams_of[0], (NI, NSAMP), 1.0, 6.0, ((0, 2), (1, 64))),
        "taps": normal_values(streams_of[1], (TAPS, NFFT), 0.5, 3.0, (), jnp.float32),
    }


def dft_table(length):
    half = length // 2
    kidx = jnp.arange(half, dtype=jnp.int32)[:, None]
    nidx = jnp.arange(length, dtype=jnp.int32)[None, :]
    phase = (kidx * nidx % length).astype(jnp.float32) * (2.0 * math.pi / length)
    norm = 1.0 / math.sqrt(length)
    return jnp.stack([jnp.cos(phase) * norm, -jnp.sin(phase) * norm], axis=1).astype(jnp.bfloat16)

def reference(raw, taps):
    blk = math.gcd(NI, 64)
    frames = raw.reshape(NI // blk, blk, NSPEC, NFFT)
    table = dft_table(NFFT).astype(jnp.float32)

    def engine(block):
        padded = jnp.concatenate([jnp.zeros((blk, TAPS - 1, NFFT), jnp.bfloat16), block], axis=1)
        filtered = sum((taps[t][None, None, :] * padded[:, t:t + NSPEC, :] for t in range(TAPS)))
        filtered = filtered.astype(jnp.bfloat16).astype(jnp.float32)
        return jnp.einsum('isn,crn->crsi', filtered, table).astype(jnp.bfloat16)
    pieces = lax.map(engine, frames)
    spectra = jnp.moveaxis(pieces, 0, 3).reshape(NCH, 2, NSPEC, NI)

    def tile(channel):
        values = channel.astype(jnp.float32)
        rotated = jnp.stack([values[1], -values[0]])
        real_part = jnp.einsum('rsi,rsj->ij', values, values)
        imag_part = jnp.einsum('rsi,rsj->ij', values, rotated)
        return jnp.stack([real_part, imag_part]) / NSPEC
    return lax.map(tile, spectra)
```

```python
import functools
import math

import jax
import jax.numpy as jnp
from jax import lax
from jax.experimental import pallas as pl
from jax.experimental.pallas import tpu as pltpu
from jax.sharding import PartitionSpec as P

MESH = pl.DeviceIdType.MESH
F32 = jnp.float32
BF16 = jnp.bfloat16
CHUNK = 128
CHUNKS = 4
PARTS = 2 * CHUNKS
FRAMES = 16
NFFT = 512
TAPS = 4
GROUP = 512


def table_rows(length):
    row = jnp.arange(length, dtype=jnp.int32)[:, None]
    n = jnp.arange(length, dtype=jnp.int32)[None, :]
    place, k, z, r = row // 16, row // 8 % 2, row // 2 % 4, row % 2
    channel = 4 * (z % 2 * 32 + place) + 2 * (z // 2) + k
    phase = (channel * n % length).astype(F32) * (2.0 * math.pi / length)
    norm = 1.0 / math.sqrt(length)
    return jnp.where(r == 0, jnp.cos(phase) * norm, -jnp.sin(phase) * norm).astype(BF16)


def position():
    g, t = lax.axis_index("inp"), lax.axis_index("tm")
    return g, t, g * 2 + t // 32, t // 8 % 4, t // 2 % 4, t % 2


def device(z, x, y, c):
    return (z // 2, z % 2 * 32 + x * 8 + y * 2 + c)


def wait_for(ref, sem):
    pltpu.make_async_copy(ref, ref, sem).wait()


def turn_kernel(
    raw, taps, table, own, got_cross, got_auto,
    ext, filt, freq, at_start, after_x, after_y, turned, cross, auto, stage,
    raw_sem, tail_send, tail_recv, send_sems, recv_sems, res_send, res_recv, out_sem,
):
    g, t, z, x, y, c = position()
    after = (lax.rem(t + 1, 64), lax.rem(t + 63, 64))
    reads = []
    for i in range(CHUNKS):
        rows = pl.ds(i * CHUNK, CHUNK)
        reads.append(
            pltpu.make_async_copy(
                raw.at[rows], ext.at[rows, pl.ds(3 * NFFT, FRAMES * NFFT)], raw_sem.at[i]
            )
        )
        reads[-1].start()

    barrier = pltpu.get_barrier_semaphore()
    along_x = [(z, lax.rem(x + d, 4), y, c) for d in (1, 3, 2)]
    along_y = [(z, x, lax.rem(y + d, 4), c) for d in (1, 3, 2)]
    along_z = [
        (lax.rem(z + d, 4), x, y, lax.rem(c + e, 2))
        for d, e in ((1, 0), (3, 0), (2, 0), (1, 1), (3, 1), (2, 1), (0, 1))
    ]
    for there in along_x + along_y + along_z:
        pl.semaphore_signal(barrier, inc=1, device_id=device(*there), device_id_type=MESH)
    for other in after:
        pl.semaphore_signal(barrier, inc=1, device_id=(g, other), device_id_type=MESH)
    pl.semaphore_wait(barrier, 15)

    tails = []
    for i in range(CHUNKS):
        rows = pl.ds(i * CHUNK, CHUNK)
        tails.append(
            pltpu.make_async_remote_copy(
                src_ref=raw.at[rows, pl.ds((FRAMES - 3) * NFFT, 3 * NFFT)],
                dst_ref=ext.at[rows, pl.ds(0, 3 * NFFT)],
                send_sem=tail_send.at[i],
                recv_sem=tail_recv.at[i],
                device_id=(g, after[0]),
                device_id_type=MESH,
            )
        )
        tails[-1].start()

    to = lax.broadcasted_iota(jnp.int32, (256, 256), 0)
    fro = lax.broadcasted_iota(jnp.int32, (256, 256), 1)
    swap = jnp.where((to // 16 == fro % 16) & (to % 16 == fro // 16), 1.0, 0.0).astype(BF16)

    def transform(i):
        rows = i * CHUNK

        def pair(j, _):
            for half in range(2):
                for b in range(0, CHUNK, 16):
                    total = None
                    for tap in range(TAPS):
                        at = pl.multiple_of((2 * j + half + tap) * NFFT, NFFT)
                        frame = ext[pl.ds(rows + b, 16), pl.ds(at, NFFT)].astype(F32)
                        term = taps[pl.ds(tap, 1), :] * frame
                        total = term if total is None else total + term
                    filt[pl.ds(half * CHUNK + b, 16), :] = total.astype(BF16)
            for m in range(0, NFFT, 256):
                out = lax.dot_general(
                    table[pl.ds(m, 256), :], filt[...], (((1,), (1,)), ((), ())),
                    preferred_element_type=F32,
                ).astype(BF16)
                for half in range(2):
                    freq[2 * j + half, pl.ds(m // 16, 16)] = out[
                        :, half * CHUNK : (half + 1) * CHUNK
                    ].reshape(16, 16, CHUNK)
            return 0

        reads[i].wait()
        lax.fori_loop(2, FRAMES // 2, pair, 0)
        tails[i].wait_recv()

        @pl.when(t == 0)
        def _():
            ext[pl.ds(rows, CHUNK), pl.ds(0, 3 * NFFT)] = jnp.zeros((CHUNK, 3 * NFFT), BF16)

        lax.fori_loop(0, 2, pair, 0)

        def place(d, _):
            px, py = d // 4, d % 4
            both = [freq[:, 2 * d + e].reshape(256, CHUNK) for e in range(2)]
            out = jnp.dot(swap, jnp.concatenate(both, axis=1), preferred_element_type=F32)
            out = out.astype(BF16)
            for e in range(2):
                block = out[:, e * CHUNK : (e + 1) * CHUNK].reshape(2, 4, 2, 16, CHUNK)
                for k in range(2):
                    at_start[2 * i + k, px, py, :, e] = block[k]
            return 0

        lax.fori_loop(0, 16, place, 0)

    def send(step, n, src, dst, there):
        pltpu.make_async_remote_copy(
            src_ref=src, dst_ref=dst, send_sem=send_sems.at[step, n],
            recv_sem=recv_sems.at[step, n], device_id=device(*there), device_id_type=MESH,
        ).start()

    def keep(step, n, src, dst):
        pltpu.make_async_copy(src, dst, recv_sems.at[step, n]).start()

    def step_x(n):
        for there in along_x:
            send(0, n, at_start.at[n, there[1]], after_x.at[n, x], there)
        keep(0, n, at_start.at[n, x], after_x.at[n, x])

    def step_y(n):
        wait_for(after_x.at[n], recv_sems.at[0, n])
        for there in along_y:
            send(1, n, after_x.at[n, :, there[2]], after_y.at[n, :, y], there)
        keep(1, n, after_x.at[n, :, y], after_y.at[n, :, y])

    def step_z(n):
        wait_for(after_y.at[n], recv_sems.at[1, n])
        for there in along_z:
            send(2, n, after_y.at[n, :, :, there[0], there[3]], turned.at[n, :, :, z, c], there)
        keep(2, n, after_y.at[n, :, :, z, c], turned.at[n, :, :, z, c])

    def advance(n):
        if 0 <= n < PARTS:
            step_y(n)
        if 0 <= n - 1 < PARTS:
            step_z(n - 1)

    for i in range(CHUNKS):
        transform(i)
        step_x(2 * i)
        step_x(2 * i + 1)
        if i == 2:
            advance(0)
    for n in range(1, PARTS + 1):
        advance(n)
    for n in range(PARTS):
        wait_for(turned.at[n], recv_sems.at[2, n])

    def columns(k, group, r, first, count):
        parts = [
            turned[2 * i + k, :, :, pl.ds(2 * group, 2), :, r].reshape(1024, CHUNK)
            for i in range(first, first + count)
        ]
        return jnp.concatenate(parts, axis=1)

    def product(a, b):
        return lax.dot_general(a, b, (((0,), (0,)), ((), ())), preferred_element_type=F32)

    scale = 1.0 / 1024.0
    partner = device(lax.rem(z + 2, 4), x, y, c)

    def tile(k, left, right, m):
        a0, a1 = (columns(k, left, r, 2 * m, 2) for r in range(2))
        b0, b1 = (columns(k, right, r, 0, 4) for r in range(2))
        real = (product(a0, b0) + product(a1, b1)) * scale
        imag = (product(a0, b1) - product(a1, b0)) * scale
        return real, imag

    def returned(src, dst, n):
        return pltpu.make_async_remote_copy(
            src_ref=src, dst_ref=dst, send_sem=res_send.at[n], recv_sem=res_recv.at[n],
            device_id=partner, device_id_type=MESH,
        )

    results = []
    for k in range(2):
        for m in range(2):
            rows = pl.ds(m * 256, 256)
            real, imag = tile(k, 1 - g, 1 - g, m)
            i = lax.broadcasted_iota(jnp.int32, (256, GROUP), 0) + m * 256
            j = lax.broadcasted_iota(jnp.int32, (256, GROUP), 1)
            auto[k, rows] = jnp.where(i <= j, real, imag).astype(BF16)
            results.append(returned(auto.at[k, rows], got_auto.at[k, rows], 4 * k + 2 * m))
            results[-1].start()
            real, imag = tile(k, 1 - g, g, m)
            cross[k, m, 0] = real.astype(BF16)
            cross[k, m, 1] = imag.astype(BF16)
            results.append(returned(cross.at[k, m], got_cross.at[k, m], 4 * k + 2 * m + 1))
            results[-1].start()

    writes = []
    for k in range(2):
        for m in range(2):
            for side in range(2):
                n = len(writes)
                if n >= 2:
                    writes[n - 2].wait()
                real, imag = tile(k, g, side, m)
                stage[n % 2, 0] = real
                stage[n % 2, 1] = imag
                writes.append(
                    pltpu.make_async_copy(
                        stage.at[n % 2],
                        own.at[k, :, pl.ds(m * 256, 256), pl.ds(side * GROUP, GROUP)],
                        out_sem.at[n % 2],
                    )
                )
                writes[-1].start()
    for w in writes[-2:]:
        w.wait()
    for i in range(CHUNKS):
        tails[i].wait_send()
    for n in range(PARTS):
        wait_for(at_start.at[n, pl.ds(0, 3)], send_sems.at[0, n])
        wait_for(after_x.at[n, pl.ds(0, 3)], send_sems.at[1, n])
        wait_for(after_y.at[n, :, :, pl.ds(0, 3)], send_sems.at[2, n])
        wait_for(after_y.at[n, :, :, 0, 0], send_sems.at[2, n])
    for r in results:
        r.wait()


def join_kernel(group, own, cross, auto, out):
    step = pl.program_id(0)

    @pl.when(step >= 2)
    def _():
        out[...] = own[...]

    @pl.when(step < 2)
    def _():
        upper = auto[0].astype(F32)
        lower = upper.T
        i = lax.broadcasted_iota(jnp.int32, upper.shape, 0)
        j = lax.broadcasted_iota(jnp.int32, upper.shape, 1)
        real = jnp.where(i <= j, upper, lower)
        imag = jnp.where(i > j, upper, jnp.where(i < j, -lower, 0.0))
        far = cross[0].astype(F32)
        for side in range(2):

            @pl.when(group[0] == side)
            def _():
                mine = pl.ds(side * GROUP, GROUP)
                others = (1 - side) * GROUP
                out[0, 0, :, mine] = real
                out[0, 1, :, mine] = imag
                for m in range(2):
                    for part in range(2):
                        out[0, part, pl.ds(m * 256, 256), pl.ds(others, GROUP)] = far[m, part]


def per_device(raw, taps):
    any_space = pl.BlockSpec(memory_space=pl.ANY)
    vmem = pl.BlockSpec(memory_space=pltpu.VMEM)
    parts = (PARTS, 4, 4, 4, 2, 2, 16, CHUNK)
    own, got_cross, got_auto = pl.pallas_call(
        turn_kernel,
        out_shape=(
            jax.ShapeDtypeStruct((2, 2, GROUP, 2 * GROUP), F32),
            jax.ShapeDtypeStruct((2, 2, 2, 256, GROUP), BF16),
            jax.ShapeDtypeStruct((2, GROUP, GROUP), BF16),
        ),
        in_specs=[any_space, vmem, vmem],
        out_specs=(any_space,) * 3,
        scratch_shapes=[
            pltpu.VMEM((GROUP, (FRAMES + 3) * NFFT), BF16),
            pltpu.VMEM((2 * CHUNK, NFFT), BF16),
            pltpu.VMEM((FRAMES, 32, 16, CHUNK), BF16),
            pltpu.VMEM(parts, BF16),
            pltpu.VMEM(parts, BF16),
            pltpu.VMEM(parts, BF16),
            pltpu.VMEM(parts, BF16),
            pltpu.VMEM((2, 2, 2, 256, GROUP), BF16),
            pltpu.VMEM((2, GROUP, GROUP), BF16),
            pltpu.VMEM((2, 2, 256, GROUP), F32),
            pltpu.SemaphoreType.DMA((CHUNKS,)),
            pltpu.SemaphoreType.DMA((CHUNKS,)),
            pltpu.SemaphoreType.DMA((CHUNKS,)),
            pltpu.SemaphoreType.DMA((3, PARTS)),
            pltpu.SemaphoreType.DMA((3, PARTS)),
            pltpu.SemaphoreType.DMA((8,)),
            pltpu.SemaphoreType.DMA((8,)),
            pltpu.SemaphoreType.DMA((2,)),
        ],
        compiler_params=pltpu.CompilerParams(
            collective_id=0, has_side_effects=True, vmem_limit_bytes=62 * 1024 * 1024
        ),
    )(raw, taps, table_rows(NFFT))

    group = lax.axis_index("inp").astype(jnp.int32).reshape(1)
    return pl.pallas_call(
        join_kernel,
        out_shape=jax.ShapeDtypeStruct((4, 2, GROUP, 2 * GROUP), F32),
        grid_spec=pltpu.PrefetchScalarGridSpec(
            num_scalar_prefetch=1,
            grid=(4,),
            in_specs=[
                pl.BlockSpec(
                    (1, 2, GROUP, 2 * GROUP), lambda i, s: (jnp.maximum(i - 2, 0), 0, 0, 0)
                ),
                pl.BlockSpec(
                    (1, 2, 2, 256, GROUP), lambda i, s: (jnp.minimum(i, 1), 0, 0, 0, 0)
                ),
                pl.BlockSpec((1, GROUP, GROUP), lambda i, s: (jnp.minimum(i, 1), 0, 0)),
            ],
            out_specs=pl.BlockSpec(
                (1, 2, GROUP, 2 * GROUP), lambda i, s: (lax.rem(i + 2 * (1 - s[0]), 4), 0, 0, 0)
            ),
        ),
        compiler_params=pltpu.CompilerParams(vmem_limit_bytes=48 * 1024 * 1024),
    )(group, own, got_cross, got_auto)


def solution(mesh):
    return jax.shard_map(
        per_device,
        mesh=mesh,
        in_specs=(P("inp", "tm"), P()),
        out_specs=P("tm", None, "inp", None),
        check_vma=False,
    )
```

```python
import functools
import math

import jax
import jax.numpy as jnp
import numpy as np
from jax import lax
from jax.experimental import pallas as pl
from jax.experimental.pallas import tpu as pltpu
from jax.sharding import PartitionSpec as P

MESH = pl.DeviceIdType.MESH
F32 = jnp.float32
BF16 = jnp.bfloat16
CHUNK = 128
CHUNKS = 4
PARTS = 4 * CHUNKS
FRAMES = 16
NFFT = 512
TAPS = 4
GROUP = 512
ORDERS = (
    "yzx", "xyz", "yxz", "zyx", "zxy", "xzy", "xyz", "xyz",
    "zyx", "yzx", "xyz", "xzy", "xyz", "zyx", "yxz", "zyx",
)
ARRIVALS = (
    (),
    ((0, 0), (1, 0), (3, 0),),
    ((2, 0), (4, 0), (5, 0),),
    ((1, 1), (0, 1), (6, 0), (3, 1), (7, 0), (8, 0), (9, 0), (5, 1), (10, 0), (14, 0), (11, 0), (13, 0), (6, 1), (2, 1), (15, 0), (7, 1), (4, 1), (8, 1), (9, 1), (12, 0), (11, 1), (10, 1), (13, 1), (14, 1), (15, 1), (12, 1),),
)


def table_rows(length):
    row = np.arange(length)[:, None]
    place, k, r, z = row // 16, row // 8 % 2, row // 4 % 2, row % 4
    channel = 4 * (z % 2 * 32 + place) + 2 * (z // 2) + k
    phase = (channel * np.arange(length)[None, :] % length) * (2.0 * math.pi / length)
    values = np.where(r == 0, np.cos(phase), -np.sin(phase)) / math.sqrt(length)
    return jnp.asarray(values.astype(np.float32).astype(BF16))


def position():
    g, t = lax.axis_index("inp"), lax.axis_index("tm")
    return g, t, g * 2 + t // 32, t // 8 % 4, t // 2 % 4, t % 2


def device(z, x, y, c):
    return (z // 2, z % 2 * 32 + x * 8 + y * 2 + c)


def wait_for(ref, sem):
    pltpu.make_async_copy(ref, ref, sem).wait()


def turn_kernel(
    raw, taps, table, own, got_cross, got_auto,
    ext, filt, freq, at_start, after_one, after_two, turned, cross, auto, stage,
    raw_sem, tail_send, tail_recv, send_sems, recv_sems, res_send, res_recv, out_sem, ready,
):
    g, t, z, x, y, c = position()
    after = (lax.rem(t + 1, 64), lax.rem(t + 63, 64))
    reads = []
    for i in range(CHUNKS):
        rows = pl.ds(i * CHUNK, CHUNK)
        reads.append(
            pltpu.make_async_copy(
                raw.at[rows], ext.at[rows, pl.ds(3 * NFFT, FRAMES * NFFT)], raw_sem.at[i]
            )
        )
        reads[-1].start()

    barrier = pltpu.get_barrier_semaphore()
    along_x = [(z, lax.rem(x + d, 4), y, c) for d in (1, 3, 2)]
    along_y = [(z, x, lax.rem(y + d, 4), c) for d in (1, 3, 2)]
    along_z = [
        (lax.rem(z + d, 4), x, y, lax.rem(c + e, 2))
        for d, e in ((1, 0), (3, 0), (2, 0), (1, 1), (3, 1), (2, 1), (0, 1))
    ]
    for there in along_x + along_y + along_z:
        pl.semaphore_signal(barrier, inc=1, device_id=device(*there), device_id_type=MESH)
    for other in after:
        pl.semaphore_signal(barrier, inc=1, device_id=(g, other), device_id_type=MESH)
    pl.semaphore_wait(barrier, 15)

    tails = []
    for i in range(CHUNKS):
        rows = pl.ds(i * CHUNK, CHUNK)
        tails.append(
            pltpu.make_async_remote_copy(
                src_ref=raw.at[rows, pl.ds((FRAMES - 3) * NFFT, 3 * NFFT)],
                dst_ref=ext.at[rows, pl.ds(0, 3 * NFFT)],
                send_sem=tail_send.at[i],
                recv_sem=tail_recv.at[i],
                device_id=(g, after[0]),
                device_id_type=MESH,
            )
        )
        tails[-1].start()

    to = lax.broadcasted_iota(jnp.int32, (256, 256), 0)
    fro = lax.broadcasted_iota(jnp.int32, (256, 256), 1)
    swap = jnp.where((to // 16 == fro % 16) & (to % 16 == fro // 16), 1.0, 0.0).astype(BF16)

    def transform(i):
        rows = i * CHUNK

        def pair(j, _):
            for half in range(2):
                for b in range(0, CHUNK, 16):
                    total = None
                    for tap in range(TAPS):
                        at = pl.multiple_of((2 * j + half + tap) * NFFT, NFFT)
                        frame = ext[pl.ds(rows + b, 16), pl.ds(at, NFFT)].astype(F32)
                        term = taps[pl.ds(tap, 1), :] * frame
                        total = term if total is None else total + term
                    filt[pl.ds(half * CHUNK + b, 16), :] = total.astype(BF16)
            for m in range(0, NFFT, 256):
                out = lax.dot_general(
                    table[pl.ds(m, 256), :], filt[...], (((1,), (1,)), ((), ())),
                    preferred_element_type=F32,
                ).astype(BF16)
                for half in range(2):
                    freq[2 * j + half, pl.ds(m // 16, 16)] = out[
                        :, half * CHUNK : (half + 1) * CHUNK
                    ].reshape(16, 16, CHUNK)
            return 0

        reads[i].wait()
        lax.fori_loop(2, FRAMES // 2, pair, 0)
        tails[i].wait_recv()

        @pl.when(t == 0)
        def _():
            ext[pl.ds(rows, CHUNK), pl.ds(0, 3 * NFFT)] = jnp.zeros((CHUNK, 3 * NFFT), BF16)

        lax.fori_loop(0, 2, pair, 0)

        def place(d, _):
            px, py = d // 4, d % 4
            both = [freq[:, 2 * d + e].reshape(256, CHUNK) for e in range(2)]
            out = jnp.dot(swap, jnp.concatenate(both, axis=1), preferred_element_type=F32)
            out = out.astype(BF16)
            for e in range(2):
                block = out[:, e * CHUNK : (e + 1) * CHUNK].reshape(4, 4, 16, CHUNK)
                for q in range(4):
                    at_start[4 * i + q, px, py, :, e] = block[q]
            return 0

        lax.fori_loop(0, 16, place, 0)

    def send(step, n, src, dst, there):
        pltpu.make_async_remote_copy(
            src_ref=src, dst_ref=dst, send_sem=send_sems.at[step, n],
            recv_sem=recv_sems.at[step, n], device_id=device(*there), device_id_type=MESH,
        ).start()

    def keep(step, n, src, dst):
        pltpu.make_async_copy(src, dst, recv_sems.at[step, n]).start()

    held = (at_start, after_one, after_two, turned)
    peers = {"x": along_x, "y": along_y, "z": along_z}

    def block(ref, n, dim, there):
        if dim == "x":
            return ref.at[n, there[1]]
        if dim == "y":
            return ref.at[n, :, there[2]]
        return ref.at[n, :, :, there[0], there[3]]

    def exchange(n, step):
        dim = ORDERS[n][step]
        mine = block(held[step + 1], n, dim, (z, x, y, c))
        for there in peers[dim]:
            send(step, n, block(held[step], n, dim, there), mine, there)
        keep(step, n, block(held[step], n, dim, (z, x, y, c)), mine)

    for i in range(CHUNKS):
        transform(i)
        for n in range(4 * i, 4 * i + 4):
            exchange(n, 0)
        for n, step in ARRIVALS[i]:
            wait_for(held[step + 1].at[n], recv_sems.at[step, n])
            exchange(n, step + 1)
    for n in range(PARTS):
        wait_for(turned.at[n], recv_sems.at[2, n])

    for there in along_z:
        pl.semaphore_signal(ready, inc=1, device_id=device(*there), device_id_type=MESH)
    pl.semaphore_wait(ready, 7)

    def columns(k, group, r, first, count):
        parts = [
            turned[4 * i + 2 * k + r, :, :, pl.ds(2 * group, 2)].reshape(1024, CHUNK)
            for i in range(first, first + count)
        ]
        return jnp.concatenate(parts, axis=1)

    def product(a, b):
        return lax.dot_general(a, b, (((0,), (0,)), ((), ())), preferred_element_type=F32)

    scale = 1.0 / 1024.0
    partner = device(lax.rem(z + 2, 4), x, y, c)

    def tile(k, left, right, m):
        a0, a1 = (columns(k, left, r, 2 * m, 2) for r in range(2))
        b0, b1 = (columns(k, right, r, 0, 4) for r in range(2))
        real = (product(a0, b0) + product(a1, b1)) * scale
        imag = (product(a0, b1) - product(a1, b0)) * scale
        return real, imag

    def returned(src, dst, n):
        return pltpu.make_async_remote_copy(
            src_ref=src, dst_ref=dst, send_sem=res_send.at[n], recv_sem=res_recv.at[n],
            device_id=partner, device_id_type=MESH,
        )

    results = []
    for k in range(2):
        for m in range(2):
            rows = pl.ds(m * 256, 256)
            real, imag = tile(k, 1 - g, 1 - g, m)
            i = lax.broadcasted_iota(jnp.int32, (256, GROUP), 0) + m * 256
            j = lax.broadcasted_iota(jnp.int32, (256, GROUP), 1)
            auto[k, rows] = jnp.where(i <= j, real, imag).astype(BF16)
            results.append(returned(auto.at[k, rows], got_auto.at[k, rows], 4 * k + 2 * m))
            results[-1].start()
            real, imag = tile(k, 1 - g, g, m)
            cross[k, m, 0] = real.astype(BF16)
            cross[k, m, 1] = imag.astype(BF16)
            results.append(returned(cross.at[k, m], got_cross.at[k, m], 4 * k + 2 * m + 1))
            results[-1].start()

    writes = []
    for k in range(2):
        for m in range(2):
            for side in range(2):
                n = len(writes)
                if n >= 2:
                    writes[n - 2].wait()
                real, imag = tile(k, g, side, m)
                stage[n % 2, 0] = real
                stage[n % 2, 1] = imag
                writes.append(
                    pltpu.make_async_copy(
                        stage.at[n % 2],
                        own.at[k, :, pl.ds(m * 256, 256), pl.ds(side * GROUP, GROUP)],
                        out_sem.at[n % 2],
                    )
                )
                writes[-1].start()
    for w in writes[-2:]:
        w.wait()
    for i in range(CHUNKS):
        tails[i].wait_send()
    for n in range(PARTS):
        for step in range(3):
            sent = held[step].at[n]
            if ORDERS[n][step] == "x":
                wait_for(sent.at[pl.ds(0, 3)], send_sems.at[step, n])
            elif ORDERS[n][step] == "y":
                wait_for(sent.at[:, pl.ds(0, 3)], send_sems.at[step, n])
            else:
                wait_for(sent.at[:, :, pl.ds(0, 3)], send_sems.at[step, n])
                wait_for(sent.at[:, :, 0, 0], send_sems.at[step, n])
    for r in results:
        r.wait()


def join_kernel(group, own, cross, auto, out):
    step = pl.program_id(0)

    @pl.when(step >= 2)
    def _():
        out[...] = own[...]

    @pl.when(step < 2)
    def _():
        upper = auto[0].astype(F32)
        lower = upper.T
        i = lax.broadcasted_iota(jnp.int32, upper.shape, 0)
        j = lax.broadcasted_iota(jnp.int32, upper.shape, 1)
        real = jnp.where(i <= j, upper, lower)
        imag = jnp.where(i > j, upper, jnp.where(i < j, -lower, 0.0))
        far = cross[0].astype(F32)
        for side in range(2):

            @pl.when(group[0] == side)
            def _():
                mine = pl.ds(side * GROUP, GROUP)
                others = (1 - side) * GROUP
                out[0, 0, :, mine] = real
                out[0, 1, :, mine] = imag
                for m in range(2):
                    for part in range(2):
                        out[0, part, pl.ds(m * 256, 256), pl.ds(others, GROUP)] = far[m, part]


def per_device(raw, taps):
    any_space = pl.BlockSpec(memory_space=pl.ANY)
    vmem = pl.BlockSpec(memory_space=pltpu.VMEM)
    parts = (PARTS, 4, 4, 4, 2, 16, CHUNK)
    own, got_cross, got_auto = pl.pallas_call(
        turn_kernel,
        out_shape=(
            jax.ShapeDtypeStruct((2, 2, GROUP, 2 * GROUP), F32),
            jax.ShapeDtypeStruct((2, 2, 2, 256, GROUP), BF16),
            jax.ShapeDtypeStruct((2, GROUP, GROUP), BF16),
        ),
        in_specs=[any_space, vmem, vmem],
        out_specs=(any_space,) * 3,
        scratch_shapes=[
            pltpu.VMEM((GROUP, (FRAMES + 3) * NFFT), BF16),
            pltpu.VMEM((2 * CHUNK, NFFT), BF16),
            pltpu.VMEM((FRAMES, 32, 16, CHUNK), BF16),
            pltpu.VMEM(parts, BF16),
            pltpu.VMEM(parts, BF16),
            pltpu.VMEM(parts, BF16),
            pltpu.VMEM(parts, BF16),
            pltpu.VMEM((2, 2, 2, 256, GROUP), BF16),
            pltpu.VMEM((2, GROUP, GROUP), BF16),
            pltpu.VMEM((2, 2, 256, GROUP), F32),
            pltpu.SemaphoreType.DMA((CHUNKS,)),
            pltpu.SemaphoreType.DMA((CHUNKS,)),
            pltpu.SemaphoreType.DMA((CHUNKS,)),
            pltpu.SemaphoreType.DMA((3, PARTS)),
            pltpu.SemaphoreType.DMA((3, PARTS)),
            pltpu.SemaphoreType.DMA((8,)),
            pltpu.SemaphoreType.DMA((8,)),
            pltpu.SemaphoreType.DMA((2,)),
            pltpu.SemaphoreType.REGULAR,
        ],
        compiler_params=pltpu.CompilerParams(
            collective_id=0, has_side_effects=True, vmem_limit_bytes=62 * 1024 * 1024
        ),
    )(raw, taps, table_rows(NFFT))

    group = lax.axis_index("inp").astype(jnp.int32).reshape(1)
    return pl.pallas_call(
        join_kernel,
        out_shape=jax.ShapeDtypeStruct((4, 2, GROUP, 2 * GROUP), F32),
        grid_spec=pltpu.PrefetchScalarGridSpec(
            num_scalar_prefetch=1,
            grid=(4,),
            in_specs=[
                pl.BlockSpec(
                    (1, 2, GROUP, 2 * GROUP), lambda i, s: (jnp.maximum(i - 2, 0), 0, 0, 0)
                ),
                pl.BlockSpec(
                    (1, 2, 2, 256, GROUP), lambda i, s: (jnp.minimum(i, 1), 0, 0, 0, 0)
                ),
                pl.BlockSpec((1, GROUP, GROUP), lambda i, s: (jnp.minimum(i, 1), 0, 0)),
            ],
            out_specs=pl.BlockSpec(
                (1, 2, GROUP, 2 * GROUP), lambda i, s: (lax.rem(i + 2 * (1 - s[0]), 4), 0, 0, 0)
            ),
        ),
        compiler_params=pltpu.CompilerParams(vmem_limit_bytes=48 * 1024 * 1024),
    )(group, own, got_cross, got_auto)


def solution(mesh):
    return jax.shard_map(
        per_device,
        mesh=mesh,
        in_specs=(P("inp", "tm"), P()),
        out_specs=P("tm", None, "inp", None),
        check_vma=False,
    )
```

```python
import functools
import math

import jax
import jax.numpy as jnp
import numpy as np
from jax import lax
from jax.experimental import pallas as pl
from jax.experimental.pallas import tpu as pltpu
from jax.sharding import PartitionSpec as P

MESH = pl.DeviceIdType.MESH
F32 = jnp.float32
BF16 = jnp.bfloat16
CHUNK = 128
CHUNKS = 4
PARTS = 4 * CHUNKS
FRAMES = 16
NFFT = 512
TAPS = 4
GROUP = 512
ORDERS = (
    "yzx", "xyz", "yxz", "zyx", "zxy", "xzy", "xyz", "xyz",
    "zyx", "yzx", "xyz", "xzy", "xyz", "zyx", "yxz", "zyx",
)
ARRIVALS = (
    (),
    ((0, 0), (1, 0), (3, 0),),
    ((2, 0), (4, 0), (5, 0),),
    ((1, 1), (0, 1), (6, 0), (3, 1), (7, 0), (8, 0), (9, 0), (5, 1), (10, 0), (14, 0), (11, 0), (13, 0), (6, 1), (2, 1), (15, 0), (7, 1), (4, 1), (8, 1), (9, 1), (12, 0), (11, 1), (10, 1), (13, 1), (14, 1), (15, 1), (12, 1),),
)


def table_rows(length):
    row = np.arange(length)[:, None]
    place, k, r, z = row // 16, row // 8 % 2, row // 4 % 2, row % 4
    channel = 4 * (z % 2 * 32 + place) + 2 * (z // 2) + k
    phase = (channel * np.arange(length)[None, :] % length) * (2.0 * math.pi / length)
    values = np.where(r == 0, np.cos(phase), -np.sin(phase)) / math.sqrt(length)
    return jnp.asarray(values.astype(np.float32).astype(BF16))


def position():
    g, t = lax.axis_index("inp"), lax.axis_index("tm")
    return g, t, g * 2 + t // 32, t // 8 % 4, t // 2 % 4, t % 2


def device(z, x, y, c):
    return (z // 2, z % 2 * 32 + x * 8 + y * 2 + c)


def wait_for(ref, sem):
    pltpu.make_async_copy(ref, ref, sem).wait()


def turn_kernel(
    raw, taps, table, own, got_cross, got_auto,
    ext, filt, freq, at_start, after_one, after_two, turned, cross, auto, stage,
    raw_sem, tail_send, tail_recv, send_sems, recv_sems, res_send, res_recv, out_sem, ready,
):
    g, t, z, x, y, c = position()
    after = (lax.rem(t + 1, 64), lax.rem(t + 63, 64))
    reads = []
    for i in range(CHUNKS):
        rows = pl.ds(i * CHUNK, CHUNK)
        reads.append(
            pltpu.make_async_copy(
                raw.at[rows], ext.at[rows, pl.ds(3 * NFFT, FRAMES * NFFT)], raw_sem.at[i]
            )
        )
        reads[-1].start()

    barrier = pltpu.get_barrier_semaphore()
    along_x = [(z, lax.rem(x + d, 4), y, c) for d in (1, 3, 2)]
    along_y = [(z, x, lax.rem(y + d, 4), c) for d in (1, 3, 2)]
    along_z = [
        (lax.rem(z + d, 4), x, y, lax.rem(c + e, 2))
        for d, e in ((1, 0), (3, 0), (2, 0), (1, 1), (3, 1), (2, 1), (0, 1))
    ]
    for there in along_x + along_y + along_z:
        pl.semaphore_signal(barrier, inc=1, device_id=device(*there), device_id_type=MESH)
    for other in after:
        pl.semaphore_signal(barrier, inc=1, device_id=(g, other), device_id_type=MESH)
    pl.semaphore_wait(barrier, 15)

    tails = []
    for i in range(CHUNKS):
        rows = pl.ds(i * CHUNK, CHUNK)
        tails.append(
            pltpu.make_async_remote_copy(
                src_ref=raw.at[rows, pl.ds((FRAMES - 3) * NFFT, 3 * NFFT)],
                dst_ref=ext.at[rows, pl.ds(0, 3 * NFFT)],
                send_sem=tail_send.at[i],
                recv_sem=tail_recv.at[i],
                device_id=(g, after[0]),
                device_id_type=MESH,
            )
        )
        tails[-1].start()

    to = lax.broadcasted_iota(jnp.int32, (256, 256), 0)
    fro = lax.broadcasted_iota(jnp.int32, (256, 256), 1)
    swap = jnp.where((to // 16 == fro % 16) & (to % 16 == fro // 16), 1.0, 0.0).astype(BF16)

    def transform(i):
        rows = i * CHUNK

        def pair(j, _):
            for half in range(2):
                for b in range(0, CHUNK, 16):
                    total = None
                    for tap in range(TAPS):
                        at = pl.multiple_of((2 * j + half + tap) * NFFT, NFFT)
                        frame = ext[pl.ds(rows + b, 16), pl.ds(at, NFFT)].astype(F32)
                        term = taps[pl.ds(tap, 1), :] * frame
                        total = term if total is None else total + term
                    filt[pl.ds(half * CHUNK + b, 16), :] = total.astype(BF16)
            for m in range(0, NFFT, 256):
                out = lax.dot_general(
                    table[pl.ds(m, 256), :], filt[...], (((1,), (1,)), ((), ())),
                    preferred_element_type=F32,
                ).astype(BF16)
                for half in range(2):
                    freq[2 * j + half, pl.ds(m // 16, 16)] = out[
                        :, half * CHUNK : (half + 1) * CHUNK
                    ].reshape(16, 16, CHUNK)
            return 0

        reads[i].wait()
        lax.fori_loop(2, FRAMES // 2, pair, 0)
        tails[i].wait_recv()

        @pl.when(t == 0)
        def _():
            ext[pl.ds(rows, CHUNK), pl.ds(0, 3 * NFFT)] = jnp.zeros((CHUNK, 3 * NFFT), BF16)

        lax.fori_loop(0, 2, pair, 0)

        def place(d, _):
            px, py = d // 4, d % 4
            both = [freq[:, 2 * d + e].reshape(256, CHUNK) for e in range(2)]
            out = jnp.dot(swap, jnp.concatenate(both, axis=1), preferred_element_type=F32)
            out = out.astype(BF16)
            for e in range(2):
                block = out[:, e * CHUNK : (e + 1) * CHUNK].reshape(4, 4, 16, CHUNK)
                for q in range(4):
                    at_start[4 * i + q, px, py, :, e] = block[q]
            return 0

        lax.fori_loop(0, 16, place, 0)

    def send(step, n, src, dst, there):
        pltpu.make_async_remote_copy(
            src_ref=src, dst_ref=dst, send_sem=send_sems.at[step, n],
            recv_sem=recv_sems.at[step, n], device_id=device(*there), device_id_type=MESH,
        ).start()

    def keep(step, n, src, dst):
        pltpu.make_async_copy(src, dst, recv_sems.at[step, n]).start()

    held = (at_start, after_one, after_two, turned)
    peers = {"x": along_x, "y": along_y, "z": along_z}

    def block(ref, n, dim, there):
        if dim == "x":
            return ref.at[n, there[1]]
        if dim == "y":
            return ref.at[n, :, there[2]]
        return ref.at[n, :, :, there[0], there[3]]

    def exchange(n, step):
        dim = ORDERS[n][step]
        mine = block(held[step + 1], n, dim, (z, x, y, c))
        for there in peers[dim]:
            send(step, n, block(held[step], n, dim, there), mine, there)
        keep(step, n, block(held[step], n, dim, (z, x, y, c)), mine)

    for i in range(CHUNKS):
        transform(i)
        for n in range(4 * i, 4 * i + 4):
            exchange(n, 0)
        for n, step in ARRIVALS[i]:
            wait_for(held[step + 1].at[n], recv_sems.at[step, n])
            exchange(n, step + 1)
    for n in range(PARTS):
        wait_for(turned.at[n], recv_sems.at[2, n])

    for there in along_z:
        pl.semaphore_signal(ready, inc=1, device_id=device(*there), device_id_type=MESH)
    pl.semaphore_wait(ready, 7)

    def columns(k, group, r, first, count):
        parts = [
            turned[4 * i + 2 * k + r, :, :, pl.ds(2 * group, 2)].reshape(1024, CHUNK)
            for i in range(first, first + count)
        ]
        return jnp.concatenate(parts, axis=1)

    def product(a, b):
        return lax.dot_general(a, b, (((0,), (0,)), ((), ())), preferred_element_type=F32)

    scale = 1.0 / 1024.0
    partner = device(lax.rem(z + 2, 4), x, y, c)

    def tile(k, left, right, m):
        a0, a1 = (columns(k, left, r, 2 * m, 2) for r in range(2))
        b0, b1 = (columns(k, right, r, 0, 4) for r in range(2))
        real = (product(a0, b0) + product(a1, b1)) * scale
        imag = (product(a0, b1) - product(a1, b0)) * scale
        return real, imag

    def returned(src, dst, n):
        return pltpu.make_async_remote_copy(
            src_ref=src, dst_ref=dst, send_sem=res_send.at[n], recv_sem=res_recv.at[n],
            device_id=partner, device_id_type=MESH,
        )

    results = []
    for k in range(2):
        for m in range(2):
            rows = pl.ds(m * 256, 256)
            real, imag = tile(k, 1 - g, 1 - g, m)
            i = lax.broadcasted_iota(jnp.int32, (256, GROUP), 0) + m * 256
            j = lax.broadcasted_iota(jnp.int32, (256, GROUP), 1)
            auto[k, rows] = jnp.where(i <= j, real, imag).astype(BF16)
            results.append(returned(auto.at[k, rows], got_auto.at[k, rows], 4 * k + 2 * m))
            results[-1].start()
            real, imag = tile(k, 1 - g, g, m)
            cross[k, m, 0] = real.astype(BF16)
            cross[k, m, 1] = imag.astype(BF16)
            results.append(returned(cross.at[k, m], got_cross.at[k, m], 4 * k + 2 * m + 1))
            results[-1].start()

    writes = []
    for k in range(2):
        for m in range(2):
            for side in range(2):
                n = len(writes)
                if n >= 2:
                    writes[n - 2].wait()
                real, imag = tile(k, g, side, m)
                stage[n % 2, 0] = real
                stage[n % 2, 1] = imag
                writes.append(
                    pltpu.make_async_copy(
                        stage.at[n % 2],
                        own.at[k, :, pl.ds(m * 256, 256), pl.ds(side * GROUP, GROUP)],
                        out_sem.at[n % 2],
                    )
                )
                writes[-1].start()
    for w in writes[-2:]:
        w.wait()
    for i in range(CHUNKS):
        tails[i].wait_send()
    for n in range(PARTS):
        for step in range(3):
            sent = held[step].at[n]
            if ORDERS[n][step] == "x":
                wait_for(sent.at[pl.ds(0, 3)], send_sems.at[step, n])
            elif ORDERS[n][step] == "y":
                wait_for(sent.at[:, pl.ds(0, 3)], send_sems.at[step, n])
            else:
                wait_for(sent.at[:, :, pl.ds(0, 3)], send_sems.at[step, n])
                wait_for(sent.at[:, :, 0, 0], send_sems.at[step, n])
    for r in results:
        r.wait()


def join_kernel(own, cross, auto, out, near, far, packed, mine, others, in_sem, own_sem, out_sem):
    g = lax.axis_index("inp")
    reads = []
    for k in range(2):
        reads.append(pltpu.make_async_copy(auto.at[k], packed.at[k], in_sem.at[k, 0]))
        reads.append(pltpu.make_async_copy(cross.at[k], far.at[k], in_sem.at[k, 1]))
    moves, writes = [], []
    for n in range(4):
        rows = pl.ds(n % 2 * 256, 256)
        moves.append(
            (
                pltpu.make_async_copy(own.at[n // 2, :, rows], near.at[n], own_sem.at[n]),
                pltpu.make_async_copy(near.at[n], out.at[2 * g + n // 2, :, rows], out_sem.at[0, n]),
            )
        )
    for copy in reads:
        copy.start()
    for read, _ in moves:
        read.start()
    for n in range(4):
        k, m = n // 2, n % 2
        if m == 0:
            reads[2 * k].wait()
            reads[2 * k + 1].wait()
        rows = pl.ds(m * 256, 256)
        here = packed[k, m * 256 : (m + 1) * 256, :].astype(F32)
        flip = packed[k, :, m * 256 : (m + 1) * 256].astype(F32).T
        i = lax.broadcasted_iota(jnp.int32, here.shape, 0) + m * 256
        j = lax.broadcasted_iota(jnp.int32, here.shape, 1)
        mine[n, 0] = jnp.where(i <= j, here, flip)
        mine[n, 1] = jnp.where(i > j, here, jnp.where(i < j, -flip, 0.0))
        others[n] = far[k, m].astype(F32)
        for side, held in ((g, mine), (1 - g, others)):
            columns = pl.ds(pl.multiple_of(side * GROUP, GROUP), GROUP)
            writes.append(
                pltpu.make_async_copy(
                    held.at[n],
                    out.at[2 * (1 - g) + k, :, rows, columns],
                    out_sem.at[1 + len(writes) % 2, n],
                )
            )
            writes[-1].start()
        moves[n][0].wait()
        moves[n][1].start()
    for copy in writes:
        copy.wait()
    for _, write in moves:
        write.wait()


def per_device(raw, taps):
    any_space = pl.BlockSpec(memory_space=pl.ANY)
    vmem = pl.BlockSpec(memory_space=pltpu.VMEM)
    parts = (PARTS, 4, 4, 4, 2, 16, CHUNK)
    own, got_cross, got_auto = pl.pallas_call(
        turn_kernel,
        out_shape=(
            jax.ShapeDtypeStruct((2, 2, GROUP, 2 * GROUP), F32),
            jax.ShapeDtypeStruct((2, 2, 2, 256, GROUP), BF16),
            jax.ShapeDtypeStruct((2, GROUP, GROUP), BF16),
        ),
        in_specs=[any_space, vmem, vmem],
        out_specs=(any_space,) * 3,
        scratch_shapes=[
            pltpu.VMEM((GROUP, (FRAMES + 3) * NFFT), BF16),
            pltpu.VMEM((2 * CHUNK, NFFT), BF16),
            pltpu.VMEM((FRAMES, 32, 16, CHUNK), BF16),
            pltpu.VMEM(parts, BF16),
            pltpu.VMEM(parts, BF16),
            pltpu.VMEM(parts, BF16),
            pltpu.VMEM(parts, BF16),
            pltpu.VMEM((2, 2, 2, 256, GROUP), BF16),
            pltpu.VMEM((2, GROUP, GROUP), BF16),
            pltpu.VMEM((2, 2, 256, GROUP), F32),
            pltpu.SemaphoreType.DMA((CHUNKS,)),
            pltpu.SemaphoreType.DMA((CHUNKS,)),
            pltpu.SemaphoreType.DMA((CHUNKS,)),
            pltpu.SemaphoreType.DMA((3, PARTS)),
            pltpu.SemaphoreType.DMA((3, PARTS)),
            pltpu.SemaphoreType.DMA((8,)),
            pltpu.SemaphoreType.DMA((8,)),
            pltpu.SemaphoreType.DMA((2,)),
            pltpu.SemaphoreType.REGULAR,
        ],
        compiler_params=pltpu.CompilerParams(
            collective_id=0, has_side_effects=True, vmem_limit_bytes=62 * 1024 * 1024
        ),
    )(raw, taps, table_rows(NFFT))

    return pl.pallas_call(
        join_kernel,
        out_shape=jax.ShapeDtypeStruct((4, 2, GROUP, 2 * GROUP), F32),
        in_specs=[any_space] * 3,
        out_specs=any_space,
        scratch_shapes=[
            pltpu.VMEM((4, 2, 256, 2 * GROUP), F32),
            pltpu.VMEM((2, 2, 2, 256, GROUP), BF16),
            pltpu.VMEM((2, GROUP, GROUP), BF16),
            pltpu.VMEM((4, 2, 256, GROUP), F32),
            pltpu.VMEM((4, 2, 256, GROUP), F32),
            pltpu.SemaphoreType.DMA((2, 2)),
            pltpu.SemaphoreType.DMA((4,)),
            pltpu.SemaphoreType.DMA((3, 4)),
        ],
        compiler_params=pltpu.CompilerParams(vmem_limit_bytes=62 * 1024 * 1024),
    )(own, got_cross, got_auto)


def solution(mesh):
    return jax.shard_map(
        per_device,
        mesh=mesh,
        in_specs=(P("inp", "tm"), P()),
        out_specs=P("tm", None, "inp", None),
        check_vma=False,
    )
```

```python
import functools
import math

import jax
import jax.numpy as jnp
import numpy as np
from jax import lax
from jax.experimental import pallas as pl
from jax.experimental.pallas import tpu as pltpu
from jax.sharding import PartitionSpec as P

MESH = pl.DeviceIdType.MESH
F32 = jnp.float32
BF16 = jnp.bfloat16
CHUNK = 128
CHUNKS = 4
PARTS = 4 * CHUNKS
FRAMES = 16
NFFT = 512
TAPS = 4
GROUP = 512
ORDERS = (
    "xzy", "yzx", "zyx", "zyx", "xyz", "zyx", "yzx", "xyz",
    "xzy", "zxy", "xzy", "zxy", "xyz", "xyz", "xyz", "zyx",
)
PLAN = (
    ("F", 0), ("S", 0), ("S", 2), ("S", 1), ("S", 3), ("F", 1), ("S", 4), ("S", 5), ("S", 6),
    ("F", 2), ("S", 9), ("S", 8), ("S", 10), ("S", 11), ("S", 7), ("W", 0, 0), ("W", 1, 0),
    ("W", 2, 0), ("W", 3, 0), ("F", 3), ("S", 13), ("S", 12), ("S", 15), ("S", 14), ("W", 4, 0),
    ("W", 6, 0), ("W", 5, 0), ("W", 2, 1), ("W", 8, 0), ("W", 9, 0), ("W", 3, 1), ("W", 10, 0),
    ("W", 11, 0), ("W", 4, 1), ("W", 7, 0), ("W", 0, 1), ("W", 5, 1), ("W", 13, 0), ("W", 1, 1),
    ("W", 7, 1), ("W", 12, 0), ("W", 15, 0), ("W", 14, 0), ("W", 6, 1), ("W", 13, 1), ("W", 8, 1),
    ("W", 9, 1), ("W", 12, 1), ("W", 10, 1), ("W", 15, 1), ("W", 11, 1), ("W", 14, 1), ("K", 0),
    ("T", 0, 0), ("T", 0, 1), ("T", 0, 2), ("T", 0, 3), ("K", 1), ("T", 1, 0), ("T", 1, 1),
    ("T", 1, 2), ("T", 1, 3),
)


def table_rows(length):
    row = np.arange(length)[:, None]
    place, k, r, z = row // 16, row // 8 % 2, row // 4 % 2, row % 4
    channel = 4 * (z % 2 * 32 + place) + 2 * (z // 2) + k
    phase = (channel * np.arange(length)[None, :] % length) * (2.0 * math.pi / length)
    values = np.where(r == 0, np.cos(phase), -np.sin(phase)) / math.sqrt(length)
    return jnp.asarray(values.astype(np.float32).astype(BF16))


def position():
    g, t = lax.axis_index("inp"), lax.axis_index("tm")
    return g, t, g * 2 + t // 32, t // 8 % 4, t // 2 % 4, t % 2


def device(z, x, y, c):
    return (z // 2, z % 2 * 32 + x * 8 + y * 2 + c)


def wait_for(ref, sem):
    pltpu.make_async_copy(ref, ref, sem).wait()


def turn_kernel(
    raw, taps, table, own, got_cross, got_auto,
    ext, filt, freq, at_start, after_one, after_two, turned, cross, auto, stage,
    raw_sem, tail_send, tail_recv, send_sems, recv_sems, res_send, res_recv, out_sem, ready,
):
    g, t, z, x, y, c = position()
    after = (lax.rem(t + 1, 64), lax.rem(t + 63, 64))
    reads = []
    for i in range(CHUNKS):
        rows = pl.ds(i * CHUNK, CHUNK)
        reads.append(
            pltpu.make_async_copy(
                raw.at[rows], ext.at[rows, pl.ds(3 * NFFT, FRAMES * NFFT)], raw_sem.at[i]
            )
        )
        reads[-1].start()

    barrier = pltpu.get_barrier_semaphore()
    along_x = [(z, lax.rem(x + d, 4), y, c) for d in (1, 3, 2)]
    along_y = [(z, x, lax.rem(y + d, 4), c) for d in (1, 3, 2)]
    along_z = [
        (lax.rem(z + d, 4), x, y, lax.rem(c + e, 2))
        for d, e in ((1, 0), (3, 0), (2, 0), (1, 1), (3, 1), (2, 1), (0, 1))
    ]
    for there in along_x + along_y + along_z:
        pl.semaphore_signal(barrier, inc=1, device_id=device(*there), device_id_type=MESH)
    for other in after:
        pl.semaphore_signal(barrier, inc=1, device_id=(g, other), device_id_type=MESH)
    pl.semaphore_wait(barrier, 15)

    tails = []
    for i in range(CHUNKS):
        rows = pl.ds(i * CHUNK, CHUNK)
        tails.append(
            pltpu.make_async_remote_copy(
                src_ref=raw.at[rows, pl.ds((FRAMES - 3) * NFFT, 3 * NFFT)],
                dst_ref=ext.at[rows, pl.ds(0, 3 * NFFT)],
                send_sem=tail_send.at[i],
                recv_sem=tail_recv.at[i],
                device_id=(g, after[0]),
                device_id_type=MESH,
            )
        )
        tails[-1].start()

    to = lax.broadcasted_iota(jnp.int32, (256, 256), 0)
    fro = lax.broadcasted_iota(jnp.int32, (256, 256), 1)
    swap = jnp.where((to // 16 == fro % 16) & (to % 16 == fro // 16), 1.0, 0.0).astype(BF16)

    def transform(i):
        rows = i * CHUNK

        def pair(j, _):
            for half in range(2):
                for b in range(0, CHUNK, 16):
                    total = None
                    for tap in range(TAPS):
                        at = pl.multiple_of((2 * j + half + tap) * NFFT, NFFT)
                        frame = ext[pl.ds(rows + b, 16), pl.ds(at, NFFT)].astype(F32)
                        term = taps[pl.ds(tap, 1), :] * frame
                        total = term if total is None else total + term
                    filt[pl.ds(half * CHUNK + b, 16), :] = total.astype(BF16)
            for m in range(0, NFFT, 256):
                out = lax.dot_general(
                    table[pl.ds(m, 256), :], filt[...], (((1,), (1,)), ((), ())),
                    preferred_element_type=F32,
                ).astype(BF16)
                for half in range(2):
                    freq[2 * j + half, pl.ds(m // 16, 16)] = out[
                        :, half * CHUNK : (half + 1) * CHUNK
                    ].reshape(16, 16, CHUNK)
            return 0

        reads[i].wait()
        lax.fori_loop(2, FRAMES // 2, pair, 0)
        tails[i].wait_recv()

        @pl.when(t == 0)
        def _():
            ext[pl.ds(rows, CHUNK), pl.ds(0, 3 * NFFT)] = jnp.zeros((CHUNK, 3 * NFFT), BF16)

        lax.fori_loop(0, 2, pair, 0)

        def place(d, _):
            px, py = d // 4, d % 4
            both = [freq[:, 2 * d + e].reshape(256, CHUNK) for e in range(2)]
            out = jnp.dot(swap, jnp.concatenate(both, axis=1), preferred_element_type=F32)
            out = out.astype(BF16)
            for e in range(2):
                block = out[:, e * CHUNK : (e + 1) * CHUNK].reshape(4, 4, 16, CHUNK)
                for q in range(4):
                    at_start[4 * i + q, px, py, :, e] = block[q]
            return 0

        lax.fori_loop(0, 16, place, 0)

    def send(step, n, src, dst, there):
        pltpu.make_async_remote_copy(
            src_ref=src, dst_ref=dst, send_sem=send_sems.at[step, n],
            recv_sem=recv_sems.at[step, n], device_id=device(*there), device_id_type=MESH,
        ).start()

    def keep(step, n, src, dst):
        pltpu.make_async_copy(src, dst, recv_sems.at[step, n]).start()

    held = (at_start, after_one, after_two, turned)
    peers = {"x": along_x, "y": along_y, "z": along_z}

    def block(ref, n, dim, there):
        if dim == "x":
            return ref.at[n, there[1]]
        if dim == "y":
            return ref.at[n, :, there[2]]
        return ref.at[n, :, :, there[0], there[3]]

    def exchange(n, step):
        dim = ORDERS[n][step]
        mine = block(held[step + 1], n, dim, (z, x, y, c))
        for there in peers[dim]:
            send(step, n, block(held[step], n, dim, there), mine, there)
        keep(step, n, block(held[step], n, dim, (z, x, y, c)), mine)

    def columns(k, group, r, first, count):
        parts = [
            turned[4 * i + 2 * k + r, :, :, pl.ds(2 * group, 2)].reshape(1024, CHUNK)
            for i in range(first, first + count)
        ]
        return jnp.concatenate(parts, axis=1)

    def product(a, b):
        return lax.dot_general(a, b, (((0,), (0,)), ((), ())), preferred_element_type=F32)

    scale = 1.0 / 1024.0
    partner = device(lax.rem(z + 2, 4), x, y, c)

    def tile(k, left, right, m):
        a0, a1 = (columns(k, left, r, 2 * m, 2) for r in range(2))
        b0, b1 = (columns(k, right, r, 0, 4) for r in range(2))
        real = (product(a0, b0) + product(a1, b1)) * scale
        imag = (product(a0, b1) - product(a1, b0)) * scale
        return real, imag

    def returned(src, dst, n):
        return pltpu.make_async_remote_copy(
            src_ref=src, dst_ref=dst, send_sem=res_send.at[n], recv_sem=res_recv.at[n],
            device_id=partner, device_id_type=MESH,
        )

    def gather(k):
        for n in range(PARTS):
            if n // 2 % 2 == k:
                wait_for(turned.at[n], recv_sems.at[2, n])
        for there in along_z:
            pl.semaphore_signal(
                ready.at[k], inc=1, device_id=device(*there), device_id_type=MESH
            )
        pl.semaphore_wait(ready.at[k], 7)

    results = []

    def give(k, block):
        m = block // 2
        rows = pl.ds(m * 256, 256)
        if block % 2 == 0:
            real, imag = tile(k, 1 - g, 1 - g, m)
            i = lax.broadcasted_iota(jnp.int32, (256, GROUP), 0) + m * 256
            j = lax.broadcasted_iota(jnp.int32, (256, GROUP), 1)
            auto[k, rows] = jnp.where(i <= j, real, imag).astype(BF16)
            results.append(returned(auto.at[k, rows], got_auto.at[k, rows], 4 * k + block))
        else:
            real, imag = tile(k, 1 - g, g, m)
            cross[k, m, 0] = real.astype(BF16)
            cross[k, m, 1] = imag.astype(BF16)
            results.append(returned(cross.at[k, m], got_cross.at[k, m], 4 * k + block))
        results[-1].start()

    for kind, *at in PLAN:
        if kind == "F":
            transform(*at)
        elif kind == "S":
            exchange(at[0], 0)
        elif kind == "W":
            n, step = at
            wait_for(held[step + 1].at[n], recv_sems.at[step, n])
            exchange(n, step + 1)
        elif kind == "K":
            gather(*at)
        else:
            give(*at)

    writes = []
    for k in range(2):
        for m in range(2):
            for side in range(2):
                n = len(writes)
                if n >= 2:
                    writes[n - 2].wait()
                real, imag = tile(k, g, side, m)
                stage[n % 2, 0] = real
                stage[n % 2, 1] = imag
                writes.append(
                    pltpu.make_async_copy(
                        stage.at[n % 2],
                        own.at[k, :, pl.ds(m * 256, 256), pl.ds(side * GROUP, GROUP)],
                        out_sem.at[n % 2],
                    )
                )
                writes[-1].start()
    for w in writes[-2:]:
        w.wait()
    for i in range(CHUNKS):
        tails[i].wait_send()
    for n in range(PARTS):
        for step in range(3):
            sent = held[step].at[n]
            if ORDERS[n][step] == "x":
                wait_for(sent.at[pl.ds(0, 3)], send_sems.at[step, n])
            elif ORDERS[n][step] == "y":
                wait_for(sent.at[:, pl.ds(0, 3)], send_sems.at[step, n])
            else:
                wait_for(sent.at[:, :, pl.ds(0, 3)], send_sems.at[step, n])
                wait_for(sent.at[:, :, 0, 0], send_sems.at[step, n])
    for r in results:
        r.wait()


def join_kernel(own, cross, auto, out, near, far, packed, mine, others, in_sem, own_sem, out_sem):
    g = lax.axis_index("inp")
    reads = []
    for k in range(2):
        reads.append(pltpu.make_async_copy(auto.at[k], packed.at[k], in_sem.at[k, 0]))
        reads.append(pltpu.make_async_copy(cross.at[k], far.at[k], in_sem.at[k, 1]))
    moves, writes = [], []
    for n in range(4):
        rows = pl.ds(n % 2 * 256, 256)
        moves.append(
            (
                pltpu.make_async_copy(own.at[n // 2, :, rows], near.at[n], own_sem.at[n]),
                pltpu.make_async_copy(near.at[n], out.at[2 * g + n // 2, :, rows], out_sem.at[0, n]),
            )
        )
    for copy in reads:
        copy.start()
    for read, _ in moves:
        read.start()
    for n in range(4):
        k, m = n // 2, n % 2
        if m == 0:
            reads[2 * k].wait()
            reads[2 * k + 1].wait()
        rows = pl.ds(m * 256, 256)
        here = packed[k, m * 256 : (m + 1) * 256, :].astype(F32)
        flip = packed[k, :, m * 256 : (m + 1) * 256].astype(F32).T
        i = lax.broadcasted_iota(jnp.int32, here.shape, 0) + m * 256
        j = lax.broadcasted_iota(jnp.int32, here.shape, 1)
        mine[n, 0] = jnp.where(i <= j, here, flip)
        mine[n, 1] = jnp.where(i > j, here, jnp.where(i < j, -flip, 0.0))
        others[n] = far[k, m].astype(F32)
        for side, held in ((g, mine), (1 - g, others)):
            columns = pl.ds(pl.multiple_of(side * GROUP, GROUP), GROUP)
            writes.append(
                pltpu.make_async_copy(
                    held.at[n],
                    out.at[2 * (1 - g) + k, :, rows, columns],
                    out_sem.at[1 + len(writes) % 2, n],
                )
            )
            writes[-1].start()
        moves[n][0].wait()
        moves[n][1].start()
    for copy in writes:
        copy.wait()
    for _, write in moves:
        write.wait()


def per_device(raw, taps):
    any_space = pl.BlockSpec(memory_space=pl.ANY)
    vmem = pl.BlockSpec(memory_space=pltpu.VMEM)
    parts = (PARTS, 4, 4, 4, 2, 16, CHUNK)
    own, got_cross, got_auto = pl.pallas_call(
        turn_kernel,
        out_shape=(
            jax.ShapeDtypeStruct((2, 2, GROUP, 2 * GROUP), F32),
            jax.ShapeDtypeStruct((2, 2, 2, 256, GROUP), BF16),
            jax.ShapeDtypeStruct((2, GROUP, GROUP), BF16),
        ),
        in_specs=[any_space, vmem, vmem],
        out_specs=(any_space,) * 3,
        scratch_shapes=[
            pltpu.VMEM((GROUP, (FRAMES + 3) * NFFT), BF16),
            pltpu.VMEM((2 * CHUNK, NFFT), BF16),
            pltpu.VMEM((FRAMES, 32, 16, CHUNK), BF16),
            pltpu.VMEM(parts, BF16),
            pltpu.VMEM(parts, BF16),
            pltpu.VMEM(parts, BF16),
            pltpu.VMEM(parts, BF16),
            pltpu.VMEM((2, 2, 2, 256, GROUP), BF16),
            pltpu.VMEM((2, GROUP, GROUP), BF16),
            pltpu.VMEM((2, 2, 256, GROUP), F32),
            pltpu.SemaphoreType.DMA((CHUNKS,)),
            pltpu.SemaphoreType.DMA((CHUNKS,)),
            pltpu.SemaphoreType.DMA((CHUNKS,)),
            pltpu.SemaphoreType.DMA((3, PARTS)),
            pltpu.SemaphoreType.DMA((3, PARTS)),
            pltpu.SemaphoreType.DMA((8,)),
            pltpu.SemaphoreType.DMA((8,)),
            pltpu.SemaphoreType.DMA((2,)),
            pltpu.SemaphoreType.REGULAR((2,)),
        ],
        compiler_params=pltpu.CompilerParams(
            collective_id=0, has_side_effects=True, vmem_limit_bytes=62 * 1024 * 1024
        ),
    )(raw, taps, table_rows(NFFT))

    return pl.pallas_call(
        join_kernel,
        out_shape=jax.ShapeDtypeStruct((4, 2, GROUP, 2 * GROUP), F32),
        in_specs=[any_space] * 3,
        out_specs=any_space,
        scratch_shapes=[
            pltpu.VMEM((4, 2, 256, 2 * GROUP), F32),
            pltpu.VMEM((2, 2, 2, 256, GROUP), BF16),
            pltpu.VMEM((2, GROUP, GROUP), BF16),
            pltpu.VMEM((4, 2, 256, GROUP), F32),
            pltpu.VMEM((4, 2, 256, GROUP), F32),
            pltpu.SemaphoreType.DMA((2, 2)),
            pltpu.SemaphoreType.DMA((4,)),
            pltpu.SemaphoreType.DMA((3, 4)),
        ],
        compiler_params=pltpu.CompilerParams(vmem_limit_bytes=62 * 1024 * 1024),
    )(own, got_cross, got_auto)


def solution(mesh):
    return jax.shard_map(
        per_device,
        mesh=mesh,
        in_specs=(P("inp", "tm"), P()),
        out_specs=P("tm", None, "inp", None),
        check_vma=False,
    )
```

```python
import functools
import math

import jax
import jax.numpy as jnp
import numpy as np
from jax import lax
from jax.experimental import pallas as pl
from jax.experimental.pallas import tpu as pltpu
from jax.sharding import PartitionSpec as P

MESH = pl.DeviceIdType.MESH
F32 = jnp.float32
BF16 = jnp.bfloat16
CHUNK = 128
CHUNKS = 4
PARTS = 4 * CHUNKS
FRAMES = 16
NFFT = 512
TAPS = 4
GROUP = 512
ORDERS = (
    "xzy", "yzx", "zyx", "zyx", "xyz", "zyx", "yzx", "xyz",
    "xzy", "zxy", "xzy", "zxy", "xyz", "xyz", "xyz", "zyx",
)
PLAN = (
    ("F", 0), ("S", 0), ("S", 2), ("S", 1), ("S", 3), ("F", 1), ("S", 4), ("S", 5), ("S", 6),
    ("F", 2), ("S", 9), ("S", 8), ("S", 10), ("S", 11), ("S", 7), ("W", 0, 0), ("W", 1, 0),
    ("W", 2, 0), ("W", 3, 0), ("F", 3), ("S", 13), ("S", 12), ("S", 15), ("S", 14), ("W", 4, 0),
    ("W", 6, 0), ("W", 5, 0), ("W", 2, 1), ("W", 8, 0), ("W", 9, 0), ("W", 3, 1), ("W", 10, 0),
    ("W", 11, 0), ("W", 4, 1), ("W", 7, 0), ("W", 0, 1), ("W", 5, 1), ("W", 13, 0), ("W", 1, 1),
    ("W", 7, 1), ("W", 12, 0), ("W", 15, 0), ("W", 14, 0), ("W", 6, 1), ("W", 13, 1), ("W", 8, 1),
    ("W", 9, 1), ("W", 12, 1), ("W", 10, 1), ("W", 15, 1), ("W", 11, 1), ("W", 14, 1), ("K", 0),
    ("T", 0, 0), ("T", 0, 1), ("T", 0, 2), ("T", 0, 3), ("K", 1), ("T", 1, 0), ("T", 1, 1),
    ("T", 1, 2), ("T", 1, 3),
)


def table_rows(length):
    row = np.arange(length)[:, None]
    place, k, r, z = row // 16, row // 8 % 2, row // 4 % 2, row % 4
    channel = 4 * (z % 2 * 32 + place) + 2 * (z // 2) + k
    phase = (channel * np.arange(length)[None, :] % length) * (2.0 * math.pi / length)
    values = np.where(r == 0, np.cos(phase), -np.sin(phase)) / math.sqrt(length)
    return jnp.asarray(values.astype(np.float32).astype(BF16))


def position():
    g, t = lax.axis_index("inp"), lax.axis_index("tm")
    return g, t, g * 2 + t // 32, t // 8 % 4, t // 2 % 4, t % 2


def device(z, x, y, c):
    return (z // 2, z % 2 * 32 + x * 8 + y * 2 + c)


def wait_for(ref, sem):
    pltpu.make_async_copy(ref, ref, sem).wait()


def turn_kernel(
    raw, taps, rows_hbm, own, got_cross, got_auto,
    ext, table, filt, freq, at_start, after_one, after_two, turned, cross, auto, stage,
    raw_sem, table_sem, tail_send, tail_recv, send_sems, recv_sems, res_send, res_recv, out_sem, ready,
):
    g, t, z, x, y, c = position()
    after = (lax.rem(t + 1, 64), lax.rem(t + 63, 64))
    reads = []
    for i in range(CHUNKS):
        rows = pl.ds(i * CHUNK, CHUNK)
        reads.append(
            pltpu.make_async_copy(
                raw.at[rows], ext.at[rows, pl.ds(3 * NFFT, FRAMES * NFFT)], raw_sem.at[i]
            )
        )
        reads[-1].start()

    fetch = pltpu.make_async_copy(rows_hbm, table, table_sem)
    fetch.start()

    barrier = pltpu.get_barrier_semaphore()
    along_x = [(z, lax.rem(x + d, 4), y, c) for d in (1, 3, 2)]
    along_y = [(z, x, lax.rem(y + d, 4), c) for d in (1, 3, 2)]
    along_z = [
        (lax.rem(z + d, 4), x, y, lax.rem(c + e, 2))
        for d, e in ((1, 0), (3, 0), (2, 0), (1, 1), (3, 1), (2, 1), (0, 1))
    ]
    for there in along_x + along_y + along_z:
        pl.semaphore_signal(barrier, inc=1, device_id=device(*there), device_id_type=MESH)
    for other in after:
        pl.semaphore_signal(barrier, inc=1, device_id=(g, other), device_id_type=MESH)
    pl.semaphore_wait(barrier, 15)

    tails = []
    for i in range(CHUNKS):
        rows = pl.ds(i * CHUNK, CHUNK)
        tails.append(
            pltpu.make_async_remote_copy(
                src_ref=raw.at[rows, pl.ds((FRAMES - 3) * NFFT, 3 * NFFT)],
                dst_ref=ext.at[rows, pl.ds(0, 3 * NFFT)],
                send_sem=tail_send.at[i],
                recv_sem=tail_recv.at[i],
                device_id=(g, after[0]),
                device_id_type=MESH,
            )
        )
        tails[-1].start()

    to = lax.broadcasted_iota(jnp.int32, (256, 256), 0)
    fro = lax.broadcasted_iota(jnp.int32, (256, 256), 1)
    swap = jnp.where((to // 16 == fro % 16) & (to % 16 == fro // 16), 1.0, 0.0).astype(BF16)

    def transform(i):
        rows = i * CHUNK

        def pair(j, _):
            for half in range(2):
                for b in range(0, CHUNK, 16):
                    total = None
                    for tap in range(TAPS):
                        at = pl.multiple_of((2 * j + half + tap) * NFFT, NFFT)
                        frame = ext[pl.ds(rows + b, 16), pl.ds(at, NFFT)].astype(F32)
                        term = taps[pl.ds(tap, 1), :] * frame
                        total = term if total is None else total + term
                    filt[pl.ds(half * CHUNK + b, 16), :] = total.astype(BF16)
            for m in range(0, NFFT, 256):
                out = lax.dot_general(
                    table[pl.ds(m, 256), :], filt[...], (((1,), (1,)), ((), ())),
                    preferred_element_type=F32,
                ).astype(BF16)
                for half in range(2):
                    freq[2 * j + half, pl.ds(m // 16, 16)] = out[
                        :, half * CHUNK : (half + 1) * CHUNK
                    ].reshape(16, 16, CHUNK)
            return 0

        reads[i].wait()
        lax.fori_loop(2, FRAMES // 2, pair, 0)
        tails[i].wait_recv()

        @pl.when(t == 0)
        def _():
            ext[pl.ds(rows, CHUNK), pl.ds(0, 3 * NFFT)] = jnp.zeros((CHUNK, 3 * NFFT), BF16)

        lax.fori_loop(0, 2, pair, 0)

        def place(d, _):
            px, py = d // 4, d % 4
            both = [freq[:, 2 * d + e].reshape(256, CHUNK) for e in range(2)]
            out = jnp.dot(swap, jnp.concatenate(both, axis=1), preferred_element_type=F32)
            out = out.astype(BF16)
            for e in range(2):
                block = out[:, e * CHUNK : (e + 1) * CHUNK].reshape(4, 4, 16, CHUNK)
                for q in range(4):
                    at_start[4 * i + q, px, py, :, e] = block[q]
            return 0

        lax.fori_loop(0, 16, place, 0)

    def send(step, n, src, dst, there):
        pltpu.make_async_remote_copy(
            src_ref=src, dst_ref=dst, send_sem=send_sems.at[step, n],
            recv_sem=recv_sems.at[step, n], device_id=device(*there), device_id_type=MESH,
        ).start()

    def keep(step, n, src, dst):
        pltpu.make_async_copy(src, dst, recv_sems.at[step, n]).start()

    held = (at_start, after_one, after_two, turned)
    peers = {"x": along_x, "y": along_y, "z": along_z}

    def block(ref, n, dim, there):
        if dim == "x":
            return ref.at[n, there[1]]
        if dim == "y":
            return ref.at[n, :, there[2]]
        return ref.at[n, :, :, there[0], there[3]]

    def exchange(n, step):
        dim = ORDERS[n][step]
        mine = block(held[step + 1], n, dim, (z, x, y, c))
        for there in peers[dim]:
            send(step, n, block(held[step], n, dim, there), mine, there)
        keep(step, n, block(held[step], n, dim, (z, x, y, c)), mine)

    def columns(k, group, r, first, count):
        parts = [
            turned[4 * i + 2 * k + r, :, :, pl.ds(2 * group, 2)].reshape(1024, CHUNK)
            for i in range(first, first + count)
        ]
        return jnp.concatenate(parts, axis=1)

    def product(a, b):
        return lax.dot_general(a, b, (((0,), (0,)), ((), ())), preferred_element_type=F32)

    scale = 1.0 / 1024.0
    partner = device(lax.rem(z + 2, 4), x, y, c)

    def tile(k, left, right, m):
        a0, a1 = (columns(k, left, r, 2 * m, 2) for r in range(2))
        b0, b1 = (columns(k, right, r, 0, 4) for r in range(2))
        real = (product(a0, b0) + product(a1, b1)) * scale
        imag = (product(a0, b1) - product(a1, b0)) * scale
        return real, imag

    def returned(src, dst, n):
        return pltpu.make_async_remote_copy(
            src_ref=src, dst_ref=dst, send_sem=res_send.at[n], recv_sem=res_recv.at[n],
            device_id=partner, device_id_type=MESH,
        )

    def gather(k):
        for n in range(PARTS):
            if n // 2 % 2 == k:
                wait_for(turned.at[n], recv_sems.at[2, n])
        for there in along_z:
            pl.semaphore_signal(
                ready.at[k], inc=1, device_id=device(*there), device_id_type=MESH
            )
        pl.semaphore_wait(ready.at[k], 7)

    results = []

    def give(k, block):
        m = block // 2
        rows = pl.ds(m * 256, 256)
        if block % 2 == 0:
            real, imag = tile(k, 1 - g, 1 - g, m)
            i = lax.broadcasted_iota(jnp.int32, (256, GROUP), 0) + m * 256
            j = lax.broadcasted_iota(jnp.int32, (256, GROUP), 1)
            auto[k, rows] = jnp.where(i <= j, real, imag).astype(BF16)
            results.append(returned(auto.at[k, rows], got_auto.at[k, rows], 4 * k + block))
        else:
            real, imag = tile(k, 1 - g, g, m)
            cross[k, m, 0] = real.astype(BF16)
            cross[k, m, 1] = imag.astype(BF16)
            results.append(returned(cross.at[k, m], got_cross.at[k, m], 4 * k + block))
        results[-1].start()

    fetch.wait()
    for kind, *at in PLAN:
        if kind == "F":
            transform(*at)
        elif kind == "S":
            exchange(at[0], 0)
        elif kind == "W":
            n, step = at
            wait_for(held[step + 1].at[n], recv_sems.at[step, n])
            exchange(n, step + 1)
        elif kind == "K":
            gather(*at)
        else:
            give(*at)

    writes = []
    for k in range(2):
        for m in range(2):
            for side in range(2):
                n = len(writes)
                if n >= 2:
                    writes[n - 2].wait()
                real, imag = tile(k, g, side, m)
                stage[n % 2, 0] = real.astype(BF16)
                stage[n % 2, 1] = imag.astype(BF16)
                writes.append(
                    pltpu.make_async_copy(
                        stage.at[n % 2],
                        own.at[k, :, pl.ds(m * 256, 256), pl.ds(side * GROUP, GROUP)],
                        out_sem.at[n % 2],
                    )
                )
                writes[-1].start()
    for w in writes[-2:]:
        w.wait()
    for i in range(CHUNKS):
        tails[i].wait_send()
    for n in range(PARTS):
        for step in range(3):
            sent = held[step].at[n]
            if ORDERS[n][step] == "x":
                wait_for(sent.at[pl.ds(0, 3)], send_sems.at[step, n])
            elif ORDERS[n][step] == "y":
                wait_for(sent.at[:, pl.ds(0, 3)], send_sems.at[step, n])
            else:
                wait_for(sent.at[:, :, pl.ds(0, 3)], send_sems.at[step, n])
                wait_for(sent.at[:, :, 0, 0], send_sems.at[step, n])
    for r in results:
        r.wait()


def join_kernel(own, cross, auto, out, near, wide, far, packed, mine, others, in_sem, own_sem, out_sem):
    g = lax.axis_index("inp")
    reads = []
    for k in range(2):
        reads.append(pltpu.make_async_copy(auto.at[k], packed.at[k], in_sem.at[k, 0]))
        reads.append(pltpu.make_async_copy(cross.at[k], far.at[k], in_sem.at[k, 1]))
    moves, writes = [], []
    for n in range(4):
        rows = pl.ds(n % 2 * 256, 256)
        moves.append(
            (
                pltpu.make_async_copy(own.at[n // 2, :, rows], near.at[n], own_sem.at[n]),
                pltpu.make_async_copy(wide.at[n], out.at[2 * g + n // 2, :, rows], out_sem.at[0, n]),
            )
        )
    for copy in reads:
        copy.start()
    for read, _ in moves:
        read.start()
    for n in range(4):
        k, m = n // 2, n % 2
        if m == 0:
            reads[2 * k].wait()
            reads[2 * k + 1].wait()
        rows = pl.ds(m * 256, 256)
        here = packed[k, m * 256 : (m + 1) * 256, :].astype(F32)
        flip = packed[k, :, m * 256 : (m + 1) * 256].astype(F32).T
        i = lax.broadcasted_iota(jnp.int32, here.shape, 0) + m * 256
        j = lax.broadcasted_iota(jnp.int32, here.shape, 1)
        mine[n, 0] = jnp.where(i <= j, here, flip)
        mine[n, 1] = jnp.where(i > j, here, jnp.where(i < j, -flip, 0.0))
        others[n] = far[k, m].astype(F32)
        for side, held in ((g, mine), (1 - g, others)):
            columns = pl.ds(pl.multiple_of(side * GROUP, GROUP), GROUP)
            writes.append(
                pltpu.make_async_copy(
                    held.at[n],
                    out.at[2 * (1 - g) + k, :, rows, columns],
                    out_sem.at[1 + len(writes) % 2, n],
                )
            )
            writes[-1].start()
        moves[n][0].wait()
        wide[n] = near[n].astype(F32)
        moves[n][1].start()
    for copy in writes:
        copy.wait()
    for _, write in moves:
        write.wait()


def per_device(raw, taps):
    any_space = pl.BlockSpec(memory_space=pl.ANY)
    vmem = pl.BlockSpec(memory_space=pltpu.VMEM)
    parts = (PARTS, 4, 4, 4, 2, 16, CHUNK)
    own, got_cross, got_auto = pl.pallas_call(
        turn_kernel,
        out_shape=(
            jax.ShapeDtypeStruct((2, 2, GROUP, 2 * GROUP), BF16),
            jax.ShapeDtypeStruct((2, 2, 2, 256, GROUP), BF16),
            jax.ShapeDtypeStruct((2, GROUP, GROUP), BF16),
        ),
        in_specs=[any_space, vmem, any_space],
        out_specs=(any_space,) * 3,
        scratch_shapes=[
            pltpu.VMEM((GROUP, (FRAMES + 3) * NFFT), BF16),
            pltpu.VMEM((NFFT, NFFT), BF16),
            pltpu.VMEM((2 * CHUNK, NFFT), BF16),
            pltpu.VMEM((FRAMES, 32, 16, CHUNK), BF16),
            pltpu.VMEM(parts, BF16),
            pltpu.VMEM(parts, BF16),
            pltpu.VMEM(parts, BF16),
            pltpu.VMEM(parts, BF16),
            pltpu.VMEM((2, 2, 2, 256, GROUP), BF16),
            pltpu.VMEM((2, GROUP, GROUP), BF16),
            pltpu.VMEM((2, 2, 256, GROUP), BF16),
            pltpu.SemaphoreType.DMA((CHUNKS,)),
            pltpu.SemaphoreType.DMA,
            pltpu.SemaphoreType.DMA((CHUNKS,)),
            pltpu.SemaphoreType.DMA((CHUNKS,)),
            pltpu.SemaphoreType.DMA((3, PARTS)),
            pltpu.SemaphoreType.DMA((3, PARTS)),
            pltpu.SemaphoreType.DMA((8,)),
            pltpu.SemaphoreType.DMA((8,)),
            pltpu.SemaphoreType.DMA((2,)),
            pltpu.SemaphoreType.REGULAR((2,)),
        ],
        compiler_params=pltpu.CompilerParams(
            collective_id=0, has_side_effects=True, vmem_limit_bytes=62 * 1024 * 1024
        ),
    )(raw, taps, table_rows(NFFT))

    return pl.pallas_call(
        join_kernel,
        out_shape=jax.ShapeDtypeStruct((4, 2, GROUP, 2 * GROUP), F32),
        in_specs=[any_space] * 3,
        out_specs=any_space,
        scratch_shapes=[
            pltpu.VMEM((4, 2, 256, 2 * GROUP), BF16),
            pltpu.VMEM((4, 2, 256, 2 * GROUP), F32),
            pltpu.VMEM((2, 2, 2, 256, GROUP), BF16),
            pltpu.VMEM((2, GROUP, GROUP), BF16),
            pltpu.VMEM((4, 2, 256, GROUP), F32),
            pltpu.VMEM((4, 2, 256, GROUP), F32),
            pltpu.SemaphoreType.DMA((2, 2)),
            pltpu.SemaphoreType.DMA((4,)),
            pltpu.SemaphoreType.DMA((3, 4)),
        ],
        compiler_params=pltpu.CompilerParams(vmem_limit_bytes=62 * 1024 * 1024),
    )(own, got_cross, got_auto)


def solution(mesh):
    return jax.shard_map(
        per_device,
        mesh=mesh,
        in_specs=(P("inp", "tm"), P()),
        out_specs=P("tm", None, "inp", None),
        check_vma=False,
    )
```
